128 devices in a mesh: ep: 32 (over z, x, core), tp: 4 (over y).
Axes of the slice: x: 4, y: 4, z: 4, core: 2. Of those that a mesh axis runs over, the one named last changes fastest.
Arguments:
- resid: bfloat16 [8192, 1536], P('ep'), may hold values from -6 to 6
- context: bfloat16 [8192, 1536], P('ep', 'tp'), may hold values from -6 to 6
- w_out: bfloat16 [1536, 1536], P('tp'), may hold values from -0.15625 to 0.15625
- pre_gain: bfloat16 [1536], replicated, may hold values from 0.5 to 1.5
- final_gain: bfloat16 [1536], replicated, may hold values from 0.5 to 1.5
- w_router: bfloat16 [1536, 40], replicated, may hold values from -0.03491211 to 0.03491211
- expert_ids: int32 [8192, 8], P('ep'), may hold values from 0 to 39, all different within a row; in each aligned block of 256 rows (0 to 255, 256 to 511, ...) at most 80 rows name the same one
- slot_expert: int32 [64], replicated, may hold values from 0 to 39, as said below
- copy_pick: int32 [32, 40], P('ep'), may hold values from 0 to 7
- w_gate: bfloat16 [64, 1536, 512], P('ep', None, 'tp'), may hold values from -0.15625 to 0.15625
- w_up: bfloat16 [64, 1536, 512], P('ep', None, 'tp'), may hold values from -0.15625 to 0.15625
- w_down: bfloat16 [64, 512, 1536], P('ep', 'tp'), may hold values from -0.25 to 0.25
Outputs:
- layer_out: bfloat16 [8192, 1536], P('ep')
The draws below stay inside these ranges and needn't reach their ends.
Inputs may be any that keep to these rules, and one draw needn't show every extreme that they name: `expert_ids`: each row names 8 different experts; among the rows of one index of ep no expert is named by more than 80 rows, a bound that some block reaches of them. `slot_expert`: every expert is held by at least one slot.
All inputs are finite; a program needn't handle non-finite values.
Results may differ from the reference program's by a relative error of at most 0.012.
Values may be sent and summed in bfloat16 or wider, within the bound.
A program may use at most 128 MiB of HBM per device.

```python
import math
import jax
import jax.numpy as jnp
import numpy as np
from jax import lax

D = 1536
FF = 512
EXPERTS = 40
TOP = 8
ROWS_DEV = 256
CAP = 80
SLOTS = 64
ROWS = 8192
N_EP = 32
N_TP = 4


def draw_slot_expert(key, part):
    order = jax.random.permutation(key, SLOTS)
    return (order % EXPERTS).astype(jnp.int32)


def touch_ends(drawn, key, smallest, high):
    shape = drawn.shape
    index_at = [jax.random.randint(jax.random.fold_in(key, axis), (), 0, shape[axis]) for axis in range(len(shape))]
    drawn = drawn.at[tuple(index_at)].set(smallest)
    longest = shape.index(max(shape))
    index_at[longest] = (index_at[longest] + 1) % shape[longest]
    return drawn.at[tuple(index_at)].set(high)


def block_scale(key, shape, shards, smallest, high):
    def one(dim, parts):
        draws = jax.random.uniform(jax.random.fold_in(jax.random.fold_in(key, 6), dim), (parts,), jnp.float32, smallest / len(shards), high / len(shards))
        return jnp.repeat(jnp.exp(draws), shape[dim] // parts).reshape((-1,) + (1,) * (len(shape) - dim - 1))

    factor_of = one(*shards[0])
    for cut in shards[1:]:
        factor_of = factor_of * one(*cut)
    return factor_of


def deal_out(key, own, number, rows, count, top, most, slope):
    ranking = jax.random.permutation(key, count)
    heavy_load, common = load_shares(count, rows * top, most, slope, True), load_shares(count, rows * top, most, slope, False)
    places = jnp.arange(count)

    def named(lengths, offset_by):
        used = int((lengths > 0).sum())
        fixed = max(1, used // 4)
        shifted = fixed + (places - fixed + offset_by * (used - fixed)) % max(1, count - fixed)
        return jnp.zeros((count,), jnp.int32).at[ranking[jnp.where(places < fixed, places, shifted)]].set(jnp.asarray(lengths, jnp.int32))

    lengths = jnp.where(number % 4 == 0, named(heavy_load, number // 4), named(common, number - number // 4 - 1))
    mixed = jax.random.permutation(jax.random.fold_in(own, 3), count)
    donor, sink = mixed[0:count // 2 * 2:2], mixed[1:count // 2 * 2:2]
    margin = jnp.minimum(lengths[donor] - 1, most - lengths[sink]) // 2
    margin = jnp.where((donor == ranking[0]) | (sink == ranking[0]) | (lengths[sink] == 0), 0, jnp.maximum(margin, 0))
    shifted = jax.random.randint(jax.random.fold_in(own, 4), (count // 2,), 0, 1 << 20) % (margin + 1)
    lengths = lengths.at[donor].add(-shifted).at[sink].add(shifted)
    members = jnp.searchsorted(jnp.cumsum(lengths), jnp.arange(rows * top), side="right").astype(jnp.int32)
    listing = members.reshape(top, rows).T
    listing = listing[jax.random.permutation(jax.random.fold_in(own, 1), rows)]
    offset_by = jax.random.randint(jax.random.fold_in(own, 2), (rows, 1), 0, top)
    return jnp.take_along_axis(listing, (jnp.arange(top)[None, :] + offset_by) % top, axis=1)


def load_shares(number_of, total, most, skew, full):
    loads = [(1 << 20) // math.isqrt(grade ** skew) + 1 for grade in range(1, number_of + 1)]
    largest = most if full else min(most, max(-(-total // number_of), total * loads[0] // sum(loads)))
    least = 1 if total - largest >= number_of - 1 else 0
    counts, surplus = [largest] + [least] * (number_of - 1), total - largest - least * (number_of - 1)
    while surplus > 0:
        free = [i for i in range(1, number_of) if counts[i] < largest] or [i for i in range(1, number_of) if counts[i] < most]
        mass, budget = sum([loads[i] for i in free]), surplus
        for i in free:
            more = min(most - counts[i], max(1, budget * loads[i] // mass), surplus)
            counts[i] = counts[i] + more
            surplus = surplus - more
    return np.array(counts)


def bell_draw(rng, extent, width, most, shards=(), kind=jnp.bfloat16):
    factor_of = block_scale(rng, extent, shards, -0.22, 0.18) if shards else 1.0
    drawn = jax.random.normal(rng, extent, jnp.float32) * width * factor_of
    return jnp.minimum(jnp.maximum(drawn, -most), most).astype(kind)


def setup_inputs(seed: int = 0) -> dict:
    seeds = jax.random.split(jax.random.key(seed), 13)
    resid = bell_draw(seeds[0], (ROWS, D), 1.0, 6.0, ((0, 32),))
    context = bell_draw(seeds[1], (ROWS, D), 1.0, 6.0, ((0, 32), (1, 4)))
    w_out = bell_draw(seeds[2], (D, D), D ** -0.5, 0.15625, ((0, 4),))
    pre_gain = jnp.clip(1.0 + 0.1 * jax.random.normal(seeds[3], (D,), jnp.float32), 0.5, 1.5).astype(jnp.bfloat16)
    final_gain = jnp.clip(1.0 + 0.1 * jax.random.normal(seeds[4], (D,), jnp.float32), 0.5, 1.5).astype(jnp.bfloat16)
    w_router = jnp.clip(jax.random.uniform(seeds[5], (D, EXPERTS), jnp.float32, -0.03491211, 0.03491211), -0.03491211, 0.03491211).astype(jnp.bfloat16)
    expert_ids_keys = jax.random.split(jax.random.fold_in(seeds[6], 1), ROWS // ROWS_DEV)
    expert_ids_turns = jax.random.permutation(jax.random.fold_in(seeds[6], 3), ROWS // ROWS_DEV)
    expert_ids = jax.vmap(lambda own, number: deal_out(jax.random.fold_in(seeds[6], 2), own, number, ROWS_DEV, EXPERTS, TOP, CAP, 1))(expert_ids_keys, expert_ids_turns).reshape((ROWS, TOP))
    slot_expert = draw_slot_expert(jax.random.fold_in(seeds[12], 71), 0)
    copy_pick = touch_ends(jax.random.randint(seeds[8], (N_EP, EXPERTS), 0, 8), jax.random.fold_in(seeds[8], 1), 0, 7).astype(jnp.int32)
    w_gate = bell_draw(seeds[9], (SLOTS, D, FF), D ** -0.5, 0.15625, ((0, 32), (2, 4)))
    w_up = bell_draw(seeds[10], (SLOTS, D, FF), D ** -0.5, 0.15625, ((0, 32), (2, 4)))
    w_down = bell_draw(seeds[11], (SLOTS, FF, D), FF ** -0.5, 0.25, ((0, 32), (1, 4)))
    return dict(resid=resid, context=context, w_out=w_out, pre_gain=pre_gain, final_gain=final_gain, w_router=w_router, expert_ids=expert_ids, slot_expert=slot_expert, copy_pick=copy_pick, w_gate=w_gate, w_up=w_up, w_down=w_down)


EPSILON = 1e-06

def rms_scaled(values, gain):
    mean_square = lax.optimization_barrier(jnp.mean(values * values, axis=-1, keepdims=True))
    return values * lax.rsqrt(mean_square + EPSILON) * gain.astype(jnp.float32)

def slot_of_pick(slot_expert, copy_pick, experts):
    count = slot_expert.shape[0]
    order = jnp.arange(count, dtype=jnp.int32)
    same = slot_expert[:, None] == slot_expert[None, :]
    before = order[None, :] < order[:, None]
    rank = lax.optimization_barrier(jnp.sum((same & before).astype(jnp.int32), axis=1))
    holds = slot_expert[None, :] == jnp.arange(experts, dtype=jnp.int32)[:, None]
    copies = lax.optimization_barrier(jnp.sum(holds.astype(jnp.int32), axis=1))
    wanted = copy_pick % copies[None, :]
    match = holds[None, :, :] & (rank[None, None, :] == wanted[:, :, None])
    return lax.optimization_barrier(jnp.sum(match.astype(jnp.int32) * order[None, None, :], axis=2))

def reference(resid, context, w_out, pre_gain, final_gain, w_router, expert_ids, slot_expert, copy_pick, w_gate, w_up, w_down):
    total_rows = resid.shape[0]
    attention = jnp.dot(context, w_out, preferred_element_type=jnp.float32)
    middle = resid.astype(jnp.float32) + attention
    normed = rms_scaled(middle, pre_gain).astype(jnp.bfloat16)
    logits = jnp.dot(normed, w_router, preferred_element_type=jnp.float32)
    chosen = jnp.take_along_axis(logits, expert_ids, axis=1)
    raised = jnp.exp(chosen)
    weights = (raised / lax.optimization_barrier(jnp.sum(raised, axis=1, keepdims=True))).astype(jnp.bfloat16)
    table = slot_of_pick(slot_expert, copy_pick, EXPERTS)
    owner = (jnp.arange(total_rows, dtype=jnp.int32) // ROWS_DEV).astype(jnp.int32)
    slot = table[owner[:, None], expert_ids].reshape(-1)
    flat_row = (jnp.arange(total_rows * TOP, dtype=jnp.int32) // TOP).astype(jnp.int32)
    flat_weight = weights.reshape(-1).astype(jnp.float32)
    quarter = FF // N_TP
    capacity = N_EP * CAP

    def per_slot(mixture, number):
        hits = slot == number
        filled = jnp.sum(hits.astype(jnp.int32))
        picked = jnp.nonzero(hits, size=capacity, fill_value=0)[0].astype(jnp.int32)
        valid = jnp.arange(capacity, dtype=jnp.int32) < filled
        rows_in = normed[flat_row[picked]]
        gate = jnp.dot(rows_in, w_gate[number], preferred_element_type=jnp.float32)
        upper = jnp.dot(rows_in, w_up[number], preferred_element_type=jnp.float32)
        hidden = (jax.nn.silu(gate) * upper).astype(jnp.bfloat16)
        down = w_down[number]
        summed = jnp.zeros((capacity, D), jnp.float32)
        for lane in range(N_TP):
            piece = jnp.dot(hidden[:, lane * quarter:(lane + 1) * quarter], down[lane * quarter:(lane + 1) * quarter], preferred_element_type=jnp.float32)
            summed = summed + lax.optimization_barrier(piece.astype(jnp.bfloat16)).astype(jnp.float32)
        scale = jnp.where(valid, flat_weight[picked], jnp.float32(0.0))
        mixture = mixture.at[flat_row[picked]].add(summed * scale[:, None])
        return (mixture, None)
    mixture, _ = lax.scan(per_slot, jnp.zeros((total_rows, D), jnp.float32), jnp.arange(SLOTS, dtype=jnp.int32))
    return rms_scaled(middle + mixture, final_gain).astype(jnp.bfloat16)
```

```python
import functools

import jax
import jax.numpy as jnp
from jax import lax
from jax.experimental import pallas as pl
from jax.experimental.pallas import tpu as pltpu
from jax.sharding import PartitionSpec as P

EPSILON = 1e-06
MESH = pl.DeviceIdType.MESH
F32 = jnp.float32
BF16 = jnp.bfloat16

D = 1536
QR = 64
HR = 128
XW = D + 128
GROUP = 4 * HR
EXPERTS = 40
SLOTS = 64


def ds(start, size, align=None):
    return pl.ds(pl.multiple_of(start, align or size), size)


def slot_choice(slot_expert, copy_pick):
    expert = lax.broadcasted_iota(jnp.int32, (EXPERTS, SLOTS), 0)
    holds = (slot_expert == expert).astype(F32)
    before = lax.broadcasted_iota(jnp.int32, (SLOTS, SLOTS), 0) < lax.broadcasted_iota(
        jnp.int32, (SLOTS, SLOTS), 1
    )
    rank = jnp.dot(
        holds.astype(BF16), before.astype(F32).astype(BF16), preferred_element_type=F32
    )
    copies = jnp.sum(holds, axis=1, keepdims=True)
    square = (EXPERTS, EXPERTS)
    diagonal = lax.broadcasted_iota(jnp.int32, square, 0) == lax.broadcasted_iota(
        jnp.int32, square, 1
    )
    pick = jnp.sum(
        jnp.where(diagonal, copy_pick.astype(F32), 0.0), axis=1, keepdims=True
    )
    wanted = pick - copies * jnp.floor((pick + 0.5) / copies)
    return jnp.where(jnp.abs(rank - wanted) < 0.5, holds, 0.0)


def kernel(
    resid,
    context,
    w_out,
    pre_gain,
    final_gain,
    w_router,
    expert_ids,
    slot_expert,
    copy_pick,
    w_gate,
    w_up,
    w_down,
    out,
    att_send,
    att_recv,
    middle,
    xall,
    wgu,
    wd,
    hid,
    yo,
    yr,
    ys,
    bhalf,
    bfull,
    z,
    ahalf,
    afull,
    psend,
    precv,
    result,
    send_sem,
    recv_sem,
    local_sem,
):
    ep = lax.axis_index("ep")
    t = lax.axis_index("tp")
    c = ep % 2
    xx = (ep // 2) % 4
    zz = ep // 8
    a = zz * (1 - c) + xx * c
    b = xx * (1 - c) + zz * c
    stride_a = 8 - 6 * c
    stride_b = 2 + 6 * c

    def along(da, db):
        return (((a + da) % 4) * stride_a + ((b + db) % 4) * stride_b + c, t)

    core = (ep + 1 - 2 * c, t)

    def lane(dt):
        return (ep, (t + dt) % 4)

    def pos(da, db):
        return c * 16 + ((b + db) % 4) * 4 + (a + da) % 4

    def group_own(db):
        return c * 4 + (b + db) % 4

    def group_core(db):
        return (1 - c) * 4 + (a + db) % 4

    counter = [0]
    sends = []

    def send(src, dst, device):
        i = counter[0]
        counter[0] += 1
        copy = pltpu.make_async_remote_copy(
            src_ref=src,
            dst_ref=dst,
            send_sem=send_sem.at[i],
            recv_sem=recv_sem.at[i],
            device_id=device,
            device_id_type=MESH,
        )
        copy.start()
        sends.append(copy)
        return i

    def arrived(i, ref):
        pltpu.make_async_remote_copy(
            src_ref=ref,
            dst_ref=ref,
            send_sem=send_sem.at[i],
            recv_sem=recv_sem.at[i],
            device_id=core,
            device_id_type=MESH,
        ).wait_recv()

    barrier = pltpu.get_barrier_semaphore()
    partners = [core, lane(1), lane(2), lane(3)]
    partners += [along(1, 0), along(3, 0), along(0, 1), along(0, 3)]
    for partner in partners:
        pl.semaphore_signal(barrier, inc=1, device_id=partner, device_id_type=MESH)

    local = []

    def fetch(src, dst):
        copy = pltpu.make_async_copy(src, dst, local_sem.at[len(local)])
        copy.start()
        local.append(copy)

    for s in range(2):
        fetch(w_gate.at[s], wgu.at[:, pl.ds(s * 512, 128)])
        fetch(w_up.at[s], wgu.at[:, pl.ds(s * 512 + 256, 128)])
        fetch(w_down.at[s], wd.at[pl.ds(s * 256, 128), :])

    def attention(dt):
        rows = context[ds(((t + dt) % 4) * QR, QR), :]
        return jnp.dot(rows, w_out[...], preferred_element_type=F32)

    att = {}
    for k, dt in enumerate((2, 1, 3)):
        att_send[k] = attention(dt).astype(BF16)
        if k == 0:
            pl.semaphore_wait(barrier, len(partners))
        att[k] = send(att_send.at[k], att_recv.at[k], lane(dt))
    own = attention(0)
    sel = slot_choice(slot_expert[...], copy_pick[...])
    for k in (1, 2, 0):
        arrived(att[k], att_recv.at[k])
        own = own + att_recv[k].astype(F32)
    mid = resid[ds(t * QR, QR), :].astype(F32) + own
    middle[...] = mid
    square = jnp.mean(mid * mid, axis=-1, keepdims=True)
    normed = (mid * lax.rsqrt(square + EPSILON) * pre_gain[...].astype(F32)).astype(BF16)
    logits = jnp.dot(normed, w_router[...], preferred_element_type=F32)
    ids = expert_ids[ds(t * QR, QR), :]
    expert = lax.broadcasted_iota(jnp.int32, (QR, EXPERTS), 1)
    named = ids[:, 0:1] == expert
    for k in range(1, 8):
        named = named | (ids[:, k : k + 1] == expert)
    raised = jnp.where(named, jnp.exp(jnp.where(named, logits, 0.0)), 0.0)
    weights = (raised / jnp.sum(raised, axis=1, keepdims=True)).astype(BF16)
    by_slot = jnp.dot(weights, sel.astype(BF16), preferred_element_type=F32).astype(BF16)

    mine = pos(0, 0)
    half = ds(mine * HR + (t // 2) * QR, QR)
    xall[half, pl.ds(0, D)] = normed
    xall[half, pl.ds(D, 128)] = jnp.concatenate(
        [by_slot, jnp.zeros((QR, 128 - SLOTS), BF16)], axis=1
    )
    i = send(xall.at[half, :], xall.at[half, :], lane(2))
    odd = t % 2
    wi = []
    for s, nb in ((0, lane(1 + 2 * odd)), (1, lane(3 - 2 * odd))):
        wi.append(
            (
                send(w_gate.at[s], wgu.at[:, pl.ds(s * 512 + 128, 128)], nb),
                wgu.at[:, pl.ds(s * 512 + 128, 128)],
            )
        )
        wi.append(
            (
                send(w_up.at[s], wgu.at[:, pl.ds(s * 512 + 384, 128)], nb),
                wgu.at[:, pl.ds(s * 512 + 384, 128)],
            )
        )
        wi.append(
            (
                send(w_down.at[s], wd.at[pl.ds(s * 256 + 128, 128), :], nb),
                wd.at[pl.ds(s * 256 + 128, 128), :],
            )
        )
    arrived(i, xall.at[ds(mine * HR + (1 - t // 2) * QR, QR), :])

    def block(p):
        return xall.at[ds(p * HR, HR), :]

    def part(p, h):
        return xall.at[ds(p * HR + h * QR, QR), :]

    def spread(p, device):
        return send(block(p), block(p), device)

    def spread_half(p, h, device):
        return send(part(p, h), part(p, h), device)

    def pos_core(da, db):
        return (1 - c) * 16 + ((a + db) % 4) * 4 + (b + da) % 4

    a_up, a_down, b_up, b_down = along(1, 0), along(3, 0), along(0, 1), along(0, 3)
    i_a0 = spread(mine, a_up)
    i_a1 = spread(mine, a_down)
    i_b0, i_b1, i_c, i_h0, i_h1 = {}, {}, {}, {}, {}

    def to_b(da):
        p = pos(da, 0)
        i_b0[da] = spread(p, b_up)
        i_b1[da] = spread(p, b_down)
        i_c[da, 0] = spread(p, core)

    def from_b(da):
        p = pos(da, 3)
        arrived(i_b0[da], block(p))
        i_h0[da] = spread_half(p, 0, b_up)
        i_c[da, 3] = spread(p, core)
        p = pos(da, 1)
        arrived(i_b1[da], block(p))
        i_h1[da] = spread_half(p, 1, b_down)
        i_c[da, 1] = spread(p, core)

    def far_b(da):
        p = pos(da, 2)
        arrived(i_h0[da], part(p, 0))
        arrived(i_h1[da], part(p, 1))
        i_c[da, 2] = spread(p, core)

    lanes = lax.broadcasted_iota(jnp.int32, (256, 128), 1)

    def hidden_of(group):
        @pl.loop(0, 2)
        def _(step):
            rows = ds(group * GROUP + step * 256, 256)
            by = xall[rows, pl.ds(D, 128)].astype(F32)
            for s in range(2):
                scale = jnp.sum(
                    jnp.where(lanes == ep * 2 + s, by, 0.0), axis=1, keepdims=True
                )
                both = jnp.dot(
                    xall[rows, pl.ds(0, D)],
                    wgu[:, pl.ds(s * 512, 512)],
                    preferred_element_type=F32,
                )
                gate, upper = both[:, :256], both[:, 256:]
                value = gate / (1.0 + jnp.exp(-gate)) * upper * scale
                hid[rows, pl.ds(s * 256, 256)] = value.astype(BF16)

    def core_group(db):
        for da in (0, 3, 1, 2):
            arrived(i_c[da, db], block(pos_core(da, db)))
        hidden_of(group_core(db))

    to_b(0)
    arrived(i_a0, block(pos(3, 0)))
    i_ah0 = spread_half(pos(3, 0), 0, a_up)
    to_b(3)
    arrived(i_a1, block(pos(1, 0)))
    i_ah1 = spread_half(pos(1, 0), 1, a_down)
    to_b(1)
    from_b(0)
    arrived(i_ah0, part(pos(2, 0), 0))
    arrived(i_ah1, part(pos(2, 0), 1))
    to_b(2)
    for copy in local:
        copy.wait()
    from_b(3)
    from_b(1)
    from_b(2)
    for j, ref in wi:
        arrived(j, ref)
    hidden_of(group_own(0))
    core_group(0)
    far_b(0)
    hidden_of(group_own(3))
    far_b(3)
    hidden_of(group_own(1))
    far_b(1)
    core_group(3)
    far_b(2)
    core_group(1)
    hidden_of(group_own(2))
    core_group(2)

    def down(group, dst):
        @pl.loop(0, 6)
        def _(step):
            rows = (step // 3) * 256
            columns = ds((step % 3) * 512, 512)
            value = jnp.dot(
                hid[ds(group * GROUP + rows, 256), :],
                wd[:, columns],
                preferred_element_type=F32,
            )
            dst[ds(rows, 256), columns] = value.astype(dst.dtype)

    def add_blocks(count, body):
        @pl.loop(0, count)
        def _(step):
            body(step)

    order = (2, 1, 3, 0)
    i_y = []
    for k, db in enumerate(order):
        down(group_core(db), yo.at[k])
        i_y.append(send(yo.at[k], yr.at[k], core))
    ranked = (2, 1, 3, 0)
    i_bh0, i_bh1 = {}, {}
    i_bf = {0: {}, 1: {}}

    def rows_of(da, h=None):
        at = ((a + da) % 4) * HR
        return ds(at, HR) if h is None else ds(at + h * QR, QR)

    for k, db in enumerate(order):
        down(group_own(db), ys.at[k])
        arrived(i_y[k], yr.at[k])
        if k == 0:
            for da in ranked:
                for h in range(2):
                    rows = rows_of(da, h)
                    ys[k, rows, :] = (ys[k, rows, :].astype(F32) + yr[k, rows, :].astype(F32)).astype(BF16)
                    if h == 0:
                        i_bh0[da] = send(ys.at[k, rows, :], bhalf.at[0, rows_of(da, 0), :], b_up)
                    else:
                        i_bh1[da] = send(ys.at[k, rows, :], bhalf.at[1, rows_of(da, 1), :], b_down)
        elif k < 3:
            h, ids_h, device = ((0, i_bh0, b_up), (1, i_bh1, b_down))[k - 1]
            for da in ranked:
                arrived(ids_h[da], bhalf.at[h, rows_of(da, h), :])
                rows = rows_of(da, h)
                ys[k, rows, :] = (
                    ys[k, rows, :].astype(F32)
                    + yr[k, rows, :].astype(F32)
                    + bhalf[h, rows, :].astype(F32)
                ).astype(BF16)
                rows = rows_of(da, 1 - h)
                ys[k, rows, :] = (ys[k, rows, :].astype(F32) + yr[k, rows, :].astype(F32)).astype(BF16)
                i_bf[h][da] = send(
                    ys.at[k, rows_of(da), :], bfull.at[h, rows_of(da), :], device
                )
    i_zh = {}
    for j, da in enumerate(ranked):
        rows = rows_of(da)
        for h in range(2):
            arrived(i_bf[h][da], bfull.at[h, rows, :])
        total = (
            ys[3, rows, :].astype(F32)
            + yr[3, rows, :].astype(F32)
            + bfull[0, rows, :].astype(F32)
            + bfull[1, rows, :].astype(F32)
        )
        if j == 0:
            z[j] = total.astype(BF16)
            i_zh[0] = send(z.at[j, pl.ds(0, QR), :], ahalf.at[0], a_up)
            i_zh[1] = send(z.at[j, pl.ds(QR, QR), :], ahalf.at[1], a_down)
        elif j < 3:
            h, device = ((0, a_up), (1, a_down))[j - 1]
            arrived(i_zh[h], ahalf.at[h])
            z[j, pl.ds((1 - h) * QR, QR), :] = total[(1 - h) * QR : (2 - h) * QR].astype(BF16)
            z[j, pl.ds(h * QR, QR), :] = (
                total[h * QR : (h + 1) * QR] + ahalf[h].astype(F32)
            ).astype(BF16)
            i_zh[2 + h] = send(z.at[j], afull.at[h], device)
        else:
            for h in range(2):
                arrived(i_zh[2 + h], afull.at[h])
            final = total + afull[0].astype(F32) + afull[1].astype(F32)

    upper_half = (t // 2).astype(F32)
    mine_rows = final[:QR] * (1.0 - upper_half) + final[QR:] * upper_half
    psend[...] = (final[:QR] * upper_half + final[QR:] * (1.0 - upper_half)).astype(BF16)
    i = send(psend, precv, lane(2))
    arrived(i, precv)
    value = middle[...] + (mine_rows + precv[...].astype(F32))
    square = jnp.mean(value * value, axis=-1, keepdims=True)
    value = value * lax.rsqrt(square + EPSILON) * final_gain[...].astype(F32)
    mine_out = ds(t * QR, QR)
    result[mine_out, :] = value.astype(BF16)
    i_out = [send(result.at[mine_out, :], result.at[mine_out, :], lane(dt)) for dt in (2, 1, 3)]
    for i, dt in zip(i_out, (2, 3, 1)):
        arrived(i, result.at[ds(((t + dt) % 4) * QR, QR), :])
    out[...] = result[...]
    for copy in sends:
        copy.wait_send()


COPIES = 128


def local(
    resid,
    context,
    w_out,
    pre_gain,
    final_gain,
    w_router,
    expert_ids,
    slot_expert,
    copy_pick,
    w_gate,
    w_up,
    w_down,
):
    vmem = pl.BlockSpec(memory_space=pltpu.VMEM)
    hbm = pl.BlockSpec(memory_space=pl.ANY)
    return pl.pallas_call(
        kernel,
        out_shape=jax.ShapeDtypeStruct((4 * QR, D), BF16),
        in_specs=[vmem] * 9 + [hbm] * 3,
        out_specs=vmem,
        scratch_shapes=[
            pltpu.VMEM((3, QR, D), BF16),
            pltpu.VMEM((3, QR, D), BF16),
            pltpu.VMEM((QR, D), F32),
            pltpu.VMEM((32 * HR, XW), BF16),
            pltpu.VMEM((D, 1024), BF16),
            pltpu.VMEM((512, D), BF16),
            pltpu.VMEM((32 * HR, 512), BF16),
            pltpu.VMEM((4, GROUP, D), BF16),
            pltpu.VMEM((4, GROUP, D), BF16),
            pltpu.VMEM((4, GROUP, D), BF16),
            pltpu.VMEM((2, GROUP, D), BF16),
            pltpu.VMEM((2, GROUP, D), BF16),
            pltpu.VMEM((3, HR, D), BF16),
            pltpu.VMEM((2, QR, D), BF16),
            pltpu.VMEM((2, HR, D), BF16),
            pltpu.VMEM((QR, D), BF16),
            pltpu.VMEM((QR, D), BF16),
            pltpu.VMEM((4 * QR, D), BF16),
            pltpu.SemaphoreType.DMA((COPIES,)),
            pltpu.SemaphoreType.DMA((COPIES,)),
            pltpu.SemaphoreType.DMA((6,)),
        ],
        compiler_params=pltpu.CompilerParams(
            collective_id=0, has_side_effects=True, vmem_limit_bytes=63 * 1024 * 1024
        ),
    )(
        resid,
        context,
        w_out,
        pre_gain[None, :],
        final_gain[None, :],
        w_router,
        expert_ids,
        slot_expert[None, :],
        copy_pick,
        w_gate,
        w_up,
        w_down,
    )


def solution(mesh):
    return jax.shard_map(
        local,
        mesh=mesh,
        in_specs=(
            P("ep", None),
            P("ep", "tp"),
            P("tp", None),
            P(),
            P(),
            P(),
            P("ep", None),
            P(),
            P("ep", None),
            P("ep", None, "tp"),
            P("ep", None, "tp"),
            P("ep", "tp", None),
        ),
        out_specs=P("ep", None),
        check_vma=False,
    )
```

```python
import functools

import jax
import jax.numpy as jnp
from jax import lax
from jax.experimental import pallas as pl
from jax.experimental.pallas import tpu as pltpu
from jax.sharding import PartitionSpec as P

EPSILON = 1e-06
MESH = pl.DeviceIdType.MESH
F32 = jnp.float32
BF16 = jnp.bfloat16

D = 1536
QR = 64
SR = QR // 2
XW = D + 128
GROUP = 4 * QR
EXPERTS = 40
SLOTS = 64


def ds(start, size, align=None):
    return pl.ds(pl.multiple_of(start, align or size), size)


def slot_choice(slot_expert, copy_pick):
    expert = lax.broadcasted_iota(jnp.int32, (EXPERTS, SLOTS), 0)
    holds = (slot_expert == expert).astype(F32)
    before = lax.broadcasted_iota(jnp.int32, (SLOTS, SLOTS), 0) < lax.broadcasted_iota(
        jnp.int32, (SLOTS, SLOTS), 1
    )
    rank = jnp.dot(
        holds.astype(BF16), before.astype(F32).astype(BF16), preferred_element_type=F32
    )
    copies = jnp.sum(holds, axis=1, keepdims=True)
    square = (EXPERTS, EXPERTS)
    diagonal = lax.broadcasted_iota(jnp.int32, square, 0) == lax.broadcasted_iota(
        jnp.int32, square, 1
    )
    pick = jnp.sum(
        jnp.where(diagonal, copy_pick.astype(F32), 0.0), axis=1, keepdims=True
    )
    wanted = pick - copies * jnp.floor((pick + 0.5) / copies)
    return jnp.where(jnp.abs(rank - wanted) < 0.5, holds, 0.0)


def kernel(
    resid,
    context,
    w_out,
    pre_gain,
    final_gain,
    w_router,
    expert_ids,
    slot_expert,
    copy_pick,
    w_gate,
    w_up,
    w_down,
    out,
    att_send,
    att_half,
    att_full,
    middle,
    relay,
    xall,
    wgu,
    wd,
    hid,
    yo,
    yr,
    ys,
    bhalf,
    bfull,
    z,
    ahalf,
    afull,
    psend,
    precv,
    send_sem,
    recv_sem,
    local_sem,
):
    ep = lax.axis_index("ep")
    t = lax.axis_index("tp")
    c = ep % 2
    xx = (ep // 2) % 4
    zz = ep // 8
    a = zz * (1 - c) + xx * c
    b = xx * (1 - c) + zz * c
    stride_a = 8 - 6 * c
    stride_b = 2 + 6 * c
    quarter = (t // 2, 1 - t // 2)

    def along(da, db):
        return (((a + da) % 4) * stride_a + ((b + db) % 4) * stride_b + c, t)

    core = (ep + 1 - 2 * c, t)
    a_up, a_down, b_up, b_down = along(1, 0), along(3, 0), along(0, 1), along(0, 3)

    def lane(dt):
        return (ep, (t + dt) % 4)

    counter = [0]
    sends = []

    def send(src, dst, device):
        i = counter[0]
        counter[0] += 1
        copy = pltpu.make_async_remote_copy(
            src_ref=src,
            dst_ref=dst,
            send_sem=send_sem.at[i],
            recv_sem=recv_sem.at[i],
            device_id=device,
            device_id_type=MESH,
        )
        copy.start()
        sends.append(copy)
        return i

    def arrived(i, ref):
        pltpu.make_async_remote_copy(
            src_ref=ref,
            dst_ref=ref,
            send_sem=send_sem.at[i],
            recv_sem=recv_sem.at[i],
            device_id=core,
            device_id_type=MESH,
        ).wait_recv()

    barrier = pltpu.get_barrier_semaphore()
    partners = [lane(1), lane(3), lane(2), core, a_up, a_down, b_up, b_down]
    for partner in partners:
        pl.semaphore_signal(barrier, inc=1, device_id=partner, device_id_type=MESH)

    local = []

    def fetch(src, dst):
        copy = pltpu.make_async_copy(src, dst, local_sem.at[len(local)])
        copy.start()
        local.append(copy)

    for s in range(2):
        fetch(w_gate.at[s], wgu.at[0, :, pl.ds(s * 256, 128)])
        fetch(w_up.at[s], wgu.at[0, :, pl.ds(s * 256 + 128, 128)])
        fetch(w_down.at[s], wd.at[pl.ds(s * 128, 128), :])

    def attention(dt):
        rows = context[ds(((t + dt) % 4) * QR, QR), :]
        return jnp.dot(rows, w_out[...], preferred_element_type=F32)

    low, high = pl.ds(0, SR), pl.ds(SR, SR)
    att_send[0] = attention(2).astype(BF16)
    pl.semaphore_wait(barrier, len(partners))
    i_0 = send(att_send.at[0, low], att_half.at[0], lane(1))
    i_1 = send(att_send.at[0, high], att_half.at[1], lane(3))
    near = attention(1)
    att_send[1, high] = near[SR:].astype(BF16)
    other = attention(3)
    att_send[2, low] = other[:SR].astype(BF16)
    own = attention(0)
    sel = slot_choice(slot_expert[...], copy_pick[...])
    arrived(i_0, att_half.at[0])
    att_send[1, low] = (near[:SR] + att_half[0].astype(F32)).astype(BF16)
    i_0 = send(att_send.at[1], att_full.at[0], lane(1))
    arrived(i_1, att_half.at[1])
    att_send[2, high] = (other[SR:] + att_half[1].astype(F32)).astype(BF16)
    i_1 = send(att_send.at[2], att_full.at[1], lane(3))
    mid = resid[ds(t * QR, QR), :].astype(F32) + own
    ids = expert_ids[:, 0:QR]
    for q in range(1, 4):
        ids = jnp.where(t == q, expert_ids[:, q * QR : (q + 1) * QR], ids)
    expert = lax.broadcasted_iota(jnp.int32, (EXPERTS, QR), 0)
    named = ids[0:1] == expert
    for k in range(1, 8):
        named = named | (ids[k : k + 1] == expert)
    arrived(i_0, att_full.at[0])
    arrived(i_1, att_full.at[1])
    mid = mid + att_full[0].astype(F32) + att_full[1].astype(F32)
    middle[...] = mid
    square = jnp.mean(mid * mid, axis=-1, keepdims=True)
    normed = (mid * lax.rsqrt(square + EPSILON) * pre_gain[...].astype(F32)).astype(BF16)
    logits = lax.dot_general(
        w_router[...], normed, (((1,), (1,)), ((), ())), preferred_element_type=F32
    )
    raised = jnp.where(named, jnp.exp(jnp.where(named, logits, 0.0)), 0.0)
    weights = (raised / jnp.sum(raised, axis=0, keepdims=True)).astype(BF16)
    by_slot = lax.dot_general(
        weights, sel.astype(BF16), (((0,), (0,)), ((), ())), preferred_element_type=F32
    ).astype(BF16)

    def pos(da, db):
        return c * 16 + ((b + db) % 4) * 4 + (a + da) % 4

    def pos_core(da, db):
        return (1 - c) * 16 + ((a + db) % 4) * 4 + (b + da) % 4

    def group_own(q, db):
        return quarter[q] * 8 + c * 4 + (b + db) % 4

    def group_core(q, db):
        return quarter[q] * 8 + (1 - c) * 4 + (a + db) % 4

    def block(q, p):
        return xall.at[ds((quarter[q] * 32 + p) * QR, QR), :]

    def part(q, p, h):
        return xall.at[ds((quarter[q] * 32 + p) * QR + h * SR, SR), :]

    def part_of_lane(dt, p, h):
        return xall.at[ds(((((t + dt) % 4) // 2) * 32 + p) * QR + h * SR, SR), :]

    mine = pos(0, 0)
    rows = ds((quarter[0] * 32 + mine) * QR, QR)
    xall[rows, pl.ds(0, D)] = normed
    xall[rows, pl.ds(D, 128)] = jnp.concatenate(
        [by_slot, jnp.zeros((QR, 128 - SLOTS), BF16)], axis=1
    )

    i_a, i_ah, i_b, i_bp, i_c = {}, {}, {}, {}, {}

    def to_b(q, da):
        ref = block(q, pos(da, 0))
        i_b[q, da, 0] = send(ref, ref, b_up)
        i_b[q, da, 1] = send(ref, ref, b_down)
        i_c[q, da, 0] = send(ref, ref, core)

    def begin(q):
        ref = block(q, mine)
        i_a[q, 0] = send(ref, ref, a_up)
        i_a[q, 1] = send(ref, ref, a_down)
        to_b(q, 0)

    def near_a(q):
        for h, da, device in ((0, 3, a_up), (1, 1, a_down)):
            arrived(i_a[q, h], block(q, pos(da, 0)))
            ref = part(q, pos(da, 0), h)
            i_ah[q, h] = send(ref, ref, device)
            to_b(q, da)

    def far_a(q):
        for h in range(2):
            arrived(i_ah[q, h], part(q, pos(2, 0), h))
        to_b(q, 2)

    def near_b(q, da):
        for h, db, device in ((0, 3, b_up), (1, 1, b_down)):
            p = pos(da, db)
            arrived(i_b[q, da, h], block(q, p))
            ref = part(q, p, h)
            i_bp[q, da, h] = send(ref, ref, device)
            i_c[q, da, db] = send(block(q, p), block(q, p), core)

    def far_b(q, da):
        p = pos(da, 2)
        for h in range(2):
            arrived(i_bp[q, da, h], part(q, p, h))
        i_c[q, da, 2] = send(block(q, p), block(q, p), core)

    lanes = lax.broadcasted_iota(jnp.int32, (GROUP, 128), 1)

    def hidden_of(items):
        for q, db, which, _ in items:
            if which == "core" and (q, db) not in ready:
                ready.add((q, db))
                for da in (0, 3, 1, 2):
                    arrived(i_c[q, da, db], block(q, pos_core(da, db)))
        groups = [
            group_own(q, db) if which == "own" else group_core(q, db)
            for q, db, which, _ in items
        ]

        @pl.loop(0, len(items))
        def _(step):
            group, side = groups[0], items[0][3]
            for j in range(1, len(items)):
                group = jnp.where(step == j, groups[j], group)
                side = jnp.where(step == j, items[j][3], side)
            rows = ds(group * GROUP, GROUP)
            both = jnp.dot(
                xall[rows, pl.ds(0, D)], wgu[side], preferred_element_type=F32
            )
            by = xall[rows, pl.ds(D, 128)].astype(F32)
            for s in range(2):
                scale = jnp.sum(
                    jnp.where(lanes == ep * 2 + s, by, 0.0), axis=1, keepdims=True
                )
                gate = both[:, s * 256 : s * 256 + 128]
                upper = both[:, s * 256 + 128 : s * 256 + 256]
                value = gate / (1.0 + jnp.exp(-gate)) * upper * scale
                hid[rows, ds(side * 256 + s * 128, 128)] = value.astype(BF16)

    ready = set()

    begin(0)
    i_0 = send(part(0, mine, 0), relay.at[0], lane(1))
    i_1 = send(part(0, mine, 1), relay.at[1], lane(3))
    arrived(i_0, relay.at[0])
    i_0 = send(relay.at[0], part_of_lane(3, mine, 0), lane(1))
    arrived(i_1, relay.at[1])
    i_1 = send(relay.at[1], part_of_lane(1, mine, 1), lane(3))
    odd = t % 2
    neighbour = (lane(1 + 2 * odd), lane(3 - 2 * odd))
    i_w = []
    for w, at in ((w_gate, 0), (w_up, 128)):
        for s in range(2):
            ref = wgu.at[1, :, pl.ds(s * 256 + at, 128)]
            i_w.append((send(w.at[s], ref, neighbour[s]), ref))
    for s in range(2):
        ref = wd.at[pl.ds(256 + s * 128, 128), :]
        i_w.append((send(w_down.at[s], ref, neighbour[s]), ref))
    near_a(0)
    arrived(i_0, part(1, mine, 0))
    arrived(i_1, part(1, mine, 1))
    begin(1)
    near_b(0, 0)
    far_a(0)
    for copy in local:
        copy.wait()
    near_b(0, 3)
    near_a(1)
    near_b(0, 1)
    near_b(0, 2)
    near_b(1, 0)
    hidden_of([(0, 0, "own", 0), (0, 0, "core", 0)])
    far_a(1)
    far_b(0, 0)
    far_b(0, 3)
    near_b(1, 3)
    far_b(0, 1)
    near_b(1, 1)
    far_b(0, 2)
    near_b(1, 2)
    hidden_of([(0, db, w, 0) for db in (3, 1) for w in ("own", "core")])
    hidden_of([(q, db, w, 0) for q, db in ((0, 2), (1, 0)) for w in ("own", "core")])
    for i, ref in i_w[:4]:
        arrived(i, ref)
    far_b(1, 0)
    hidden_of([(0, db, w, 1) for db in (2, 0) for w in ("own", "core")])
    far_b(1, 3)
    hidden_of([(0, db, w, 1) for db in (3, 1) for w in ("own", "core")])
    far_b(1, 1)
    hidden_of(
        [(1, 0, w, 1) for w in ("own", "core")]
        + [(1, 3, w, side) for w in ("own", "core") for side in range(2)]
    )
    far_b(1, 2)

    order = (2, 1, 3, 0)
    i_y = {}

    def down(group, put):
        @pl.loop(0, 3)
        def _(step):
            columns = ds(step * 512, 512)
            put(
                columns,
                jnp.dot(
                    hid[ds(group * GROUP, GROUP), :],
                    wd[:, columns],
                    preferred_element_type=F32,
                ),
            )

    def for_core(q, k):
        def put(columns, value):
            yo[q, k, :, columns] = value.astype(BF16)

        down(group_core(q, order[k]), put)
        i_y[q, k] = send(yo.at[q, k], yr.at[q, k], core)

    def for_own(q, k):
        arrived(i_y[q, k], yr.at[q, k])

        def put(columns, value):
            ys[q, k, :, columns] = (value + yr[q, k, :, columns].astype(F32)).astype(BF16)

        down(group_own(q, order[k]), put)

    i_bh, i_bf, i_z = {}, {}, {}

    def rows_of(da, h=None):
        at = ((a + da) % 4) * QR
        return ds(at, QR) if h is None else ds(at + h * SR, SR)

    def far_sums(q):
        for da in order:
            for h, device in ((0, b_up), (1, b_down)):
                rows = rows_of(da, h)
                i_bh[q, da, h] = send(ys.at[q, 0, rows], bhalf.at[q, h, rows], device)

    def near_sums(q, k):
        h, device = k - 1, (b_up, b_down)[k - 1]
        for da in order:
            rows = rows_of(da, h)
            arrived(i_bh[q, da, h], bhalf.at[q, h, rows])
            ys[q, k, rows] = (
                ys[q, k, rows].astype(F32) + bhalf[q, h, rows].astype(F32)
            ).astype(BF16)
            rows = rows_of(da)
            i_bf[q, da, h] = send(ys.at[q, k, rows], bfull.at[q, h, rows], device)

    def last_sums(q):
        for j, da in enumerate(order):
            rows = rows_of(da)
            for h in range(2):
                arrived(i_bf[q, da, h], bfull.at[q, h, rows])
            total = (
                ys[q, 3, rows].astype(F32)
                + bfull[q, 0, rows].astype(F32)
                + bfull[q, 1, rows].astype(F32)
            )
            if j == 0:
                z[q, 0] = total.astype(BF16)
                i_z[0] = send(z.at[q, 0, low], ahalf.at[q, 0], a_up)
                i_z[1] = send(z.at[q, 0, high], ahalf.at[q, 1], a_down)
            elif j < 3:
                h, device = ((0, a_up), (1, a_down))[j - 1]
                arrived(i_z[h], ahalf.at[q, h])
                added = total[h * SR : (h + 1) * SR] + ahalf[q, h].astype(F32)
                kept = total[(1 - h) * SR : (2 - h) * SR]
                z[q, j, pl.ds(h * SR, SR)] = added.astype(BF16)
                z[q, j, pl.ds((1 - h) * SR, SR)] = kept.astype(BF16)
                i_z[2 + h] = send(z.at[q, j], afull.at[q, h], device)
            else:
                for h in range(2):
                    arrived(i_z[2 + h], afull.at[q, h])
                return total + afull[q, 0].astype(F32) + afull[q, 1].astype(F32)

    for i, ref in i_w[4:]:
        arrived(i, ref)
    for_core(0, 0)
    for_core(0, 1)
    for_own(0, 0)
    far_sums(0)
    hidden_of([(1, db, w, side) for db in (1, 2) for w in ("own", "core") for side in range(2)])
    for_core(1, 0)
    for_core(1, 1)
    for_own(1, 0)
    far_sums(1)
    for_own(1, 1)
    near_sums(1, 1)
    for_core(1, 2)
    for_core(0, 2)
    for_own(1, 2)
    near_sums(1, 2)
    for_own(0, 1)
    near_sums(0, 1)
    for_own(0, 2)
    near_sums(0, 2)
    for_core(1, 3)
    for_core(0, 3)
    for_own(1, 3)
    for_own(0, 3)
    psend[...] = last_sums(1).astype(BF16)
    i_0 = send(psend, precv, lane(2))
    mixture = last_sums(0)
    arrived(i_0, precv)
    value = middle[...] + (mixture + precv[...].astype(F32))
    square = jnp.mean(value * value, axis=-1, keepdims=True)
    value = value * lax.rsqrt(square + EPSILON) * final_gain[...].astype(F32)

    def out_rows(dt):
        return out.at[ds(((t + dt) % 4) * QR, QR), :]

    def out_half(dt, h):
        return out.at[ds(((t + dt) % 4) * QR + h * SR, SR), :]

    out[ds(t * QR, QR), :] = value.astype(BF16)
    i_0 = send(out_rows(0), out_rows(0), lane(1))
    i_1 = send(out_rows(0), out_rows(0), lane(3))
    arrived(i_0, out_rows(3))
    i_0 = send(out_half(3, 0), out_half(3, 0), lane(1))
    arrived(i_1, out_rows(1))
    i_1 = send(out_half(1, 1), out_half(1, 1), lane(3))
    arrived(i_0, out_half(2, 0))
    arrived(i_1, out_half(2, 1))
    for copy in sends:
        copy.wait_send()


COPIES = 160


def local(
    resid,
    context,
    w_out,
    pre_gain,
    final_gain,
    w_router,
    expert_ids,
    slot_expert,
    copy_pick,
    w_gate,
    w_up,
    w_down,
):
    vmem = pl.BlockSpec(memory_space=pltpu.VMEM)
    hbm = pl.BlockSpec(memory_space=pl.ANY)
    return pl.pallas_call(
        kernel,
        out_shape=jax.ShapeDtypeStruct((4 * QR, D), BF16),
        in_specs=[vmem] * 9 + [hbm] * 3,
        out_specs=vmem,
        scratch_shapes=[
            pltpu.VMEM((3, QR, D), BF16),
            pltpu.VMEM((2, SR, D), BF16),
            pltpu.VMEM((2, QR, D), BF16),
            pltpu.VMEM((QR, D), F32),
            pltpu.VMEM((2, SR, XW), BF16),
            pltpu.VMEM((16 * GROUP, XW), BF16),
            pltpu.VMEM((2, D, 512), BF16),
            pltpu.VMEM((512, D), BF16),
            pltpu.VMEM((16 * GROUP, 512), BF16),
            pltpu.VMEM((2, 4, GROUP, D), BF16),
            pltpu.VMEM((2, 4, GROUP, D), BF16),
            pltpu.VMEM((2, 4, GROUP, D), BF16),
            pltpu.VMEM((2, 2, GROUP, D), BF16),
            pltpu.VMEM((2, 2, GROUP, D), BF16),
            pltpu.VMEM((2, 3, QR, D), BF16),
            pltpu.VMEM((2, 2, SR, D), BF16),
            pltpu.VMEM((2, 2, QR, D), BF16),
            pltpu.VMEM((QR, D), BF16),
            pltpu.VMEM((QR, D), BF16),
            pltpu.SemaphoreType.DMA((COPIES,)),
            pltpu.SemaphoreType.DMA((COPIES,)),
            pltpu.SemaphoreType.DMA((6,)),
        ],
        compiler_params=pltpu.CompilerParams(
            collective_id=0, has_side_effects=True, vmem_limit_bytes=63 * 1024 * 1024
        ),
    )(
        resid,
        context,
        w_out,
        pre_gain,
        final_gain,
        w_router.T,
        expert_ids.T,
        slot_expert[None, :],
        copy_pick,
        w_gate,
        w_up,
        w_down,
    )


def solution(mesh):
    return jax.shard_map(
        local,
        mesh=mesh,
        in_specs=(
            P("ep", None),
            P("ep", "tp"),
            P("tp", None),
            P(),
            P(),
            P(),
            P("ep", None),
            P(),
            P("ep", None),
            P("ep", None, "tp"),
            P("ep", None, "tp"),
            P("ep", "tp", None),
        ),
        out_specs=P("ep", None),
        check_vma=False,
    )
```
